256 devices in a mesh: dp: 32 (over x, y, core), type: 8 (over z).
Axes of the slice: x: 4, y: 4, z: 8, core: 2. Of those that a mesh axis runs over, the one named last changes fastest.
Arguments:
- tokens: bfloat16 [32768, 4096], P(('dp', 'type')), may hold values from -6 to 6
- token_types: int32 [32768, 1], P(('dp', 'type')), may hold values from 0 to 7
- tile_mask: int32 [32, 8, 8], P('dp', 'type'), may hold values from 0 to 1, as said below
- queries: bfloat16 [32768, 4096], P(('dp', 'type')), may hold values from -60 to 60
- keys: bfloat16 [32768, 4096], P(('dp', 'type')), may hold values from -4 to 4
- gate_weight: bfloat16 [8, 4096, 7168], P('type', None, 'dp'), may hold values from -0.09375 to 0.09375
- up_weight: bfloat16 [8, 4096, 7168], P('type', None, 'dp'), may hold values from -0.09375 to 0.09375
- down_weight: bfloat16 [8, 7168, 4096], P('type', 'dp'), may hold values from -0.0625 to 0.0625
Outputs:
- expert_out: bfloat16 [32768, 4096], P(('dp', 'type'))
- attended: bfloat16 [32768, 4096], P(('dp', 'type'))
The draws below stay inside these ranges and needn't reach their ends.
Inputs may be any that keep to these rules, and one draw needn't show every extreme that they name: `tile_mask`: every diagonal entry is 1.
All inputs are finite; a program needn't handle non-finite values.
Results may differ from the reference program's by a relative error of at most 0.02.
Values may be sent and summed in bfloat16 or wider, within the bound.
A program may use at most 128 MiB of HBM per device.

```python
import math
import jax
import jax.numpy as jnp
from jax import lax

D = 4096
FF = 7168
HEADS = 32
HEAD = 128
TOK_DEV = 128
EXPERTS = 8
SEQ = 1024
EVENTS = 32
TOKENS = 32768
EXP_CAP = 16
N_DP = 32
N_TYPE = 8


def query_key_pair(key):
    base = jax.random.fold_in(key, 7)
    query_key, keys_key = jax.random.split(base, 2)
    query_vals = 1.5 * jnp.clip(jax.random.normal(query_key, (TOKENS, D), jnp.float32), -6.0, 6.0)
    key_vals = jnp.clip(jax.random.normal(keys_key, (TOKENS, D), jnp.float32), -4.0, 4.0)
    return (query_vals, key_vals)


def draw_queries(key, part):
    return query_key_pair(key)[0].astype(jnp.bfloat16)


def draw_keys(key, part):
    return query_key_pair(key)[1].astype(jnp.bfloat16)


def draw_tile_mask(key, part):
    random_bits = jax.random.randint(jax.random.fold_in(key, 11), (EVENTS, N_TYPE, N_TYPE), 0, 2, jnp.int32)
    tile_ids = jnp.arange(N_TYPE, dtype=jnp.int32)
    diagonal = (tile_ids[:, None] == tile_ids[None, :]).astype(jnp.int32)
    return jnp.maximum(random_bits, diagonal[None, :, :])


def levels(stream_key, extent, cuts, least, largest):
    factor_of = 1.0
    for axis_at, parts in cuts:
        draws = jax.random.uniform(jax.random.fold_in(jax.random.fold_in(stream_key, 6), axis_at), (parts,), jnp.float32, least / len(cuts), largest / len(cuts))
        factor_of = factor_of * jnp.repeat(jnp.exp(draws), extent[axis_at] // parts).reshape((-1,) + (1,) * (len(extent) - 1 - axis_at))
    return factor_of


def picks_of(own_key, rows, amount, top, lift):
    sequence = jax.random.permutation(jax.random.fold_in(own_key, 1), amount)
    favour = sequence
    for power in range(3):
        favour = favour * favour // amount
    favour = favour * lift // amount
    lots = jax.random.randint(jax.random.fold_in(own_key, 2), (rows, amount), 0, 4096) + favour
    fixed_rows = jax.random.permutation(jax.random.fold_in(own_key, 3), rows)[jnp.arange(amount) % rows]
    lots = jnp.where(jnp.arange(rows)[:, None] == fixed_rows[None, :], 1 << 14, lots)
    priority = lots * amount + jnp.arange(amount)
    return lax.top_k(priority.astype(jnp.int32), top)[1].astype(jnp.int32)


def gaussian(rng, shape, scale, reach, cuts=(), held_as=jnp.bfloat16):
    level = levels(rng, shape, cuts, -0.22, 0.18) if cuts else 1.0
    drawn = jax.random.normal(rng, shape, jnp.float32) * scale * level
    return jnp.minimum(jnp.maximum(drawn, -reach), reach).astype(held_as)


def setup_inputs(seed: int = 0) -> dict:
    streams_of = jax.random.split(jax.random.key(seed), 9)
    return {
        "tokens": gaussian(streams_of[0], (TOKENS, D), 1.0, 6.0, ((0, 256),)),
        "token_types": picks_of(streams_of[1], TOKENS, EXPERTS, 1, 2048),
        "tile_mask": draw_tile_mask(jax.random.fold_in(streams_of[8], 71), 0),
        "queries": draw_queries(jax.random.fold_in(streams_of[8], 71), 0),
        "keys": draw_keys(jax.random.fold_in(streams_of[8], 71), 0),
        "gate_weight": gaussian(streams_of[5], (EXPERTS, D, FF), D ** -0.5, 0.09375, ((0, 8), (2, 32))),
        "up_weight": gaussian(streams_of[6], (EXPERTS, D, FF), D ** -0.5, 0.09375, ((0, 8), (2, 32))),
        "down_weight": gaussian(streams_of[7], (EXPERTS, FF, D), FF ** -0.5, 0.0625, ((0, 8), (1, 32))),
    }


def expert_block(packed_rows, gate_mat, up_mat, down_mat):
    block_width = FF // N_DP

    def accumulate(running, block_index):
        first_col = block_index * block_width
        gate_act = jnp.dot(packed_rows, lax.dynamic_slice_in_dim(gate_mat, first_col, block_width, 1), preferred_element_type=jnp.float32)
        up_act = jnp.dot(packed_rows, lax.dynamic_slice_in_dim(up_mat, first_col, block_width, 1), preferred_element_type=jnp.float32)
        hidden = (jax.nn.silu(gate_act) * up_act).astype(jnp.bfloat16)
        partial_value = jnp.dot(hidden, lax.dynamic_slice_in_dim(down_mat, first_col, block_width, 0), preferred_element_type=jnp.float32).astype(jnp.bfloat16)
        return (running + partial_value.astype(jnp.float32), None)
    combined, _ = lax.scan(accumulate, jnp.zeros((packed_rows.shape[0], D), jnp.float32), jnp.arange(N_DP, dtype=jnp.int32))
    return combined.astype(jnp.bfloat16)

def attend(query_rows, key_rows, value_rows, allowed):
    query_heads = query_rows.astype(jnp.float32).reshape(SEQ, HEADS, HEAD)
    key_heads = key_rows.astype(jnp.float32).reshape(SEQ, HEADS, HEAD)
    value_heads = value_rows.astype(jnp.float32).reshape(SEQ, HEADS, HEAD)
    scores = jnp.einsum('qhd,khd->hqk', query_heads, key_heads) * (1.0 / math.sqrt(HEAD))
    masked = jnp.where(allowed[None], scores, -jnp.inf)
    row_max = lax.optimization_barrier(jnp.max(masked, axis=-1, keepdims=True))
    weights = jnp.where(allowed[None], jnp.exp(masked - row_max), 0.0).astype(jnp.bfloat16)
    total_weight = lax.optimization_barrier(jnp.sum(weights.astype(jnp.float32), axis=-1))
    mixed_rows = jnp.einsum('hqk,khd->qhd', weights.astype(jnp.float32), value_heads) / jnp.transpose(total_weight)[:, :, None]
    return mixed_rows.reshape(SEQ, D).astype(jnp.bfloat16)

def reference(tokens, token_types, tile_mask, queries, keys, gate_weight, up_weight, down_weight):
    flat_types = token_types[:, 0].astype(jnp.int32)
    type_grid = flat_types.reshape(EVENTS, SEQ)
    one_hot = (type_grid[:, :, None] == jnp.arange(EXPERTS, dtype=jnp.int32)[None, None, :]).astype(jnp.int32)
    event_rank = lax.optimization_barrier(jnp.sum((jnp.cumsum(one_hot, axis=1, dtype=jnp.int32) - one_hot) * one_hot, axis=2, dtype=jnp.int32))
    slot_grid = jnp.arange(EVENTS, dtype=jnp.int32)[:, None] * EXP_CAP + event_rank
    slot_grid = jnp.where(event_rank < EXP_CAP, slot_grid, EVENTS * EXP_CAP)
    slot_index = slot_grid.reshape(TOKENS).astype(jnp.int32)
    packed = jnp.zeros((EXPERTS, EVENTS * EXP_CAP, D), jnp.bfloat16).at[flat_types, slot_index].set(tokens, mode='drop')
    expert_packed = lax.map(lambda packed_args: expert_block(*packed_args), (packed, gate_weight, up_weight, down_weight))
    expert_out = expert_packed.at[flat_types, slot_index].get(mode='fill', fill_value=0)
    tile_index = jnp.arange(SEQ, dtype=jnp.int32) // TOK_DEV

    def per_event(event_args):
        query_rows, key_rows, value_rows, mask_rows = event_args
        allowed = mask_rows[tile_index[:, None], tile_index[None, :]] == 1
        return attend(query_rows, key_rows, value_rows, allowed)
    attended = lax.map(per_event, (queries.reshape(EVENTS, SEQ, D), keys.reshape(EVENTS, SEQ, D), expert_out.reshape(EVENTS, SEQ, D), tile_mask))
    return (expert_out, attended.reshape(TOKENS, D))
```

```python
import math

import jax
import jax.numpy as jnp
from jax import lax
from jax.sharding import PartitionSpec as P

HEAD = 128
EXP_CAP = 16


def on_device(tokens, token_types, tile_mask, queries, keys, gate_weight, up_weight, down_weight):
    n_type = lax.axis_size("type")
    my_index = lax.axis_index("type")
    tok_rows = tokens.shape[0]
    feat_width = tokens.shape[1]
    type_ids = jnp.arange(n_type, dtype=jnp.int32)
    slot_ids = jnp.arange(EXP_CAP, dtype=jnp.int32)
    keys_all = lax.all_gather(keys, "type", axis=0, tiled=True)
    event_types = lax.all_gather(token_types[:, 0], "type", axis=0, tiled=True)
    hot = (event_types[None, :] == type_ids[:, None]).astype(jnp.int32)
    rank = jnp.cumsum(hot, axis=1) - hot
    place = (
        ((rank[:, None, :] == slot_ids[None, :, None]) & (hot[:, None, :] == 1))
        .astype(jnp.bfloat16)
        .reshape(n_type * EXP_CAP, n_type * tok_rows)
    )
    own_place = lax.dynamic_slice_in_dim(place, my_index * tok_rows, tok_rows, 1)
    contrib = jnp.dot(own_place, tokens, preferred_element_type=jnp.float32).astype(jnp.bfloat16)
    packed = lax.psum_scatter(contrib, "type", scatter_dimension=0, tiled=True)
    block_rows = lax.all_gather(packed, "dp", axis=0, tiled=True)
    gate_act = jnp.dot(block_rows, gate_weight[0], preferred_element_type=jnp.float32)
    up_act = jnp.dot(block_rows, up_weight[0], preferred_element_type=jnp.float32)
    hidden = (jax.nn.silu(gate_act) * up_act).astype(jnp.bfloat16)
    partial_terms = jnp.dot(hidden, down_weight[0], preferred_element_type=jnp.float32)
    summed = lax.psum_scatter(
        partial_terms.astype(jnp.bfloat16), "dp", scatter_dimension=0, tiled=True
    )
    slot_values = lax.all_gather(summed, "type", axis=0, tiled=True)
    expert_out = jnp.einsum(
        "pt,pd->td", own_place, slot_values, preferred_element_type=jnp.float32
    ).astype(jnp.bfloat16)
    mask_row = tile_mask[0, 0]
    allowed = jnp.repeat(mask_row == 1, tok_rows)
    head_count = feat_width // HEAD
    query_heads = queries.reshape(tok_rows, head_count, HEAD)
    key_heads = keys_all.reshape(-1, head_count, HEAD)
    value_heads = slot_values.reshape(-1, head_count, HEAD)
    scores = jnp.einsum(
        "qhd,khd->hqk", query_heads, key_heads, preferred_element_type=jnp.float32
    ) * (1.0 / math.sqrt(HEAD))
    masked = jnp.where(allowed[None, None, :], scores, -jnp.inf)
    row_max = jnp.max(masked, axis=-1, keepdims=True)
    weights = jnp.where(allowed[None, None, :], jnp.exp(masked - row_max), 0.0).astype(jnp.bfloat16)
    total_weight = jnp.sum(weights.astype(jnp.float32), axis=-1)
    slot_weights = jnp.einsum(
        "hqk,pk->hqp", weights, place, preferred_element_type=jnp.float32
    ).astype(jnp.bfloat16)
    attended = (
        jnp.einsum("hqp,phd->qhd", slot_weights, value_heads, preferred_element_type=jnp.float32)
        / jnp.transpose(total_weight)[:, :, None]
    )
    return (expert_out, attended.reshape(tok_rows, feat_width).astype(jnp.bfloat16))


def solution(mesh):
    return jax.shard_map(
        on_device,
        mesh=mesh,
        in_specs=(
            P(("dp", "type"), None),
            P(("dp", "type"), None),
            P("dp", "type", None),
            P(("dp", "type"), None),
            P(("dp", "type"), None),
            P("type", None, "dp"),
            P("type", None, "dp"),
            P("type", "dp", None),
        ),
        out_specs=(P(("dp", "type"), None), P(("dp", "type"), None)),
        check_vma=False,
    )
```

```python
import math

import jax
import jax.numpy as jnp
from jax import lax
from jax.experimental import pallas as pl
from jax.experimental.pallas import tpu as pltpu
from jax.sharding import PartitionSpec as P

MESH = pl.DeviceIdType.MESH
BF = jnp.bfloat16
F32 = jnp.float32
HEAD = 128
CAP = 16
NZ = 8
NX = 4
TOK = 128
D = 4096
HALF = D // 2
FFB = 224
GRP = D // NZ
SCALE = 1.0 / math.sqrt(HEAD)
NEG = -1e30
N_SEM = 140
EARLY_KEYS = (1, 7)


def nt(a, b):
    return lax.dot_general(a, b, (((1,), (1,)), ((), ())), preferred_element_type=F32)


def tn(a, b):
    return lax.dot_general(a, b, (((0,), (0,)), ((), ())), preferred_element_type=F32)


def kernel(
    meta_in, tok_in, q_in, k_in, wg_in, wu_in, wd_in,
    oe_out, oa_out,
    mg, tok, qs, ka, qa, sa, mb, db, rb, sb, xf, wg, wu, wd, gacc, uacc, hid,
    ps, po, pr, s0, r0, s1, r1, yb, q0, z1, q1, vf, vv, kk, st, sr, wts, okm, oe, oa,
    ssem, rsem, lsem,
):
    z = lax.axis_index("type")
    dp = lax.axis_index("dp")
    core = dp % 2
    chip = dp // 2
    y = chip % NX
    x = chip // NX
    first = x * (1 - core) + y * core
    second = y * (1 - core) + x * core

    def plane(a, b):
        px = a * (1 - core) + b * core
        py = b * (1 - core) + a * core
        return {"dp": (px * NX + py) * 2 + core}

    sib = {"dp": dp + 1 - 2 * core}
    fp = plane((first + 1) % NX, second)
    fm = plane((first + NX - 1) % NX, second)
    sp = plane(first, (second + 1) % NX)
    sm = plane(first, (second + NX - 1) % NX)
    zp = {"type": (z + 1) % NZ}
    zm = {"type": (z + NZ - 1) % NZ}

    counter = [0]
    started = []

    def send(src, dst, device):
        at = counter[0]
        counter[0] += 1
        copy = pltpu.make_async_remote_copy(
            src_ref=src, dst_ref=dst, send_sem=ssem.at[at], recv_sem=rsem.at[at],
            device_id=device, device_id_type=MESH,
        )
        copy.start()
        started.append(copy)
        return copy

    locals_at = [0]

    def fetch(src, dst):
        copy = pltpu.make_async_copy(src, dst, lsem.at[locals_at[0]])
        locals_at[0] += 1
        copy.start()
        return copy

    def cols(i, width):
        return pl.ds(pl.multiple_of(i * width, width), width)

    get_meta = fetch(meta_in, mg.at[z])
    get_tok = fetch(tok_in, tok)
    get_k = fetch(k_in.at[:, cols(z, GRP)], ka.at[z])
    get_q = fetch(q_in.at[:, cols(z, GRP)], qa.at[z])
    get_qs = fetch(q_in, qs)
    get_w = [
        fetch(wg_in.at[0], wg),
        fetch(wu_in.at[0], wu),
        fetch(wd_in.at[0, :, pl.ds(0, HALF)], wd.at[0]),
        fetch(wd_in.at[0, :, pl.ds(HALF, HALF)], wd.at[1]),
    ]

    barrier = pltpu.get_barrier_semaphore()
    peers = [{"type": (z + d) % NZ} for d in range(1, NZ)] + [sib, fp, fm, sp, sm]
    for peer in peers:
        pl.semaphore_signal(barrier, inc=1, device_id=peer, device_id_type=MESH)
    pl.semaphore_wait(barrier, len(peers))

    get_meta.wait()
    meta_copies = [send(mg.at[z], mg.at[z], {"type": (z + d) % NZ}) for d in range(1, NZ)]

    def send_slice(src, dst, d):
        to = (z + d) % NZ
        return send(src.at[:, cols(to, GRP)], dst.at[z], {"type": to})

    key_copies = [send_slice(k_in, ka, d) for d in EARLY_KEYS]

    for copy in meta_copies:
        copy.wait_recv()

    expert = lax.broadcasted_iota(jnp.int32, (CAP, TOK), 0)
    hot = [jnp.broadcast_to(mg[s, 0:1, :], (CAP, TOK)) == expert for s in range(NZ)]
    hot_rows = jnp.concatenate([h.astype(F32) for h in hot], axis=0).astype(BF)
    row = lax.broadcasted_iota(jnp.int32, (TOK, 2 * TOK), 0)
    col = lax.broadcasted_iota(jnp.int32, (TOK, 2 * TOK), 1)
    upper = jnp.where((row < col) | (col >= TOK), 1.0, 0.0).astype(BF)
    sums = jnp.dot(hot_rows, upper, preferred_element_type=F32)
    offset = jnp.zeros((CAP, TOK), F32)
    ranks = []
    for s in range(NZ):
        part = sums[s * CAP : (s + 1) * CAP]
        rank = part[:, :TOK] + offset
        ranks.append(jnp.where(hot[s], jnp.minimum(rank, 31.0), 64.0))
        offset = offset + part[:, TOK:]
    rank_rows = jnp.concatenate(ranks, axis=1).astype(BF)
    slot = lax.broadcasted_iota(jnp.int32, (TOK, CAP), 0)
    of_expert = lax.broadcasted_iota(jnp.int32, (TOK, CAP), 1)
    spread = jnp.where(slot // CAP == of_expert, 1.0, 0.0).astype(BF)
    rank_of = jnp.dot(spread, rank_rows, preferred_element_type=F32)
    wanted = (lax.broadcasted_iota(jnp.int32, (TOK, TOK), 0) % CAP).astype(F32)
    for s in range(NZ):
        place = jnp.where(rank_of[:, s * TOK : (s + 1) * TOK] == wanted, 1.0, 0.0)
        sa[s] = place.astype(BF)

    get_tok.wait()
    mine = sa[z]
    for h in range(2):
        placed = jnp.dot(mine, tok[:, h * HALF : (h + 1) * HALF], preferred_element_type=F32)
        db[h] = placed.astype(BF).reshape(NZ, CAP, HALF)
    arriving = {}
    for step in range(4):
        for h in range(2):
            for way in range(2):
                begin = 0 if h == way else 1
                if step < begin:
                    continue
                far = 4 - step
                target = (z + far) % NZ if way == 0 else (z + NZ - far) % NZ
                if step == begin:
                    src = db.at[h, target]
                else:
                    arriving[h, way].wait_recv()
                    sb[way, h, step - 1] = db[h, target] + rb[way, h, step - 1]
                    src = sb.at[way, h, step - 1]
                arriving[h, way] = send(src, rb.at[way, h, step], zp if way == 0 else zm)

    key_copies += [send_slice(k_in, ka, d) for d in range(1, NZ) if d not in EARLY_KEYS]
    query_copies = [send_slice(q_in, qa, d) for d in range(1, NZ)]

    mask_rows = jnp.concatenate([mg[s, 1:2, :] for s in range(NZ)], axis=0)
    for j in range(NZ):
        mb[j] = jnp.broadcast_to(mask_rows[:, j : j + 1], (NZ, TOK)).astype(F32)

    for h in range(2):
        arriving[h, 0].wait_recv()
        arriving[h, 1].wait_recv()
        xf[h, second, first, core] = db[h, z] + rb[0, h, 3] + rb[1, h, 3]

    def own_row(h):
        return send(xf.at[h, second, first, core], xf.at[h, first, second, core], sib)

    row_a = own_row(1 - core)
    row_b = own_row(core)
    row_a.wait_recv()

    def unit(b, a):
        return xf.at[core, b, a]

    def to_sibling(b, a):
        return send(unit(b, a), xf.at[core, a, b], sib)

    def move(ref, device):
        return send(ref, ref, device)

    from_sib = []
    a_minus, a_plus, a_far = (first + NX - 1) % NX, (first + 1) % NX, (first + 2) % NX
    b_minus, b_plus, b_far = (second + NX - 1) % NX, (second + 1) % NX, (second + 2) % NX
    near_p = move(unit(second, first), fp)
    near_m = move(unit(second, first), fm)
    beside = [(first, move(unit(second, first), sp), move(unit(second, first), sm))]
    near_p.wait_recv()
    far_p = move(xf.at[core, second, a_minus, 0], fp)
    beside.append((a_minus, move(unit(second, a_minus), sp), move(unit(second, a_minus), sm)))
    from_sib.append(to_sibling(second, a_minus))
    near_m.wait_recv()
    far_m = move(xf.at[core, second, a_plus, 1], fm)
    beside.append((a_plus, move(unit(second, a_plus), sp), move(unit(second, a_plus), sm)))
    from_sib.append(to_sibling(second, a_plus))
    opposite = []

    def relay(entry):
        a, up, down = entry
        up.wait_recv()
        half_p = move(xf.at[core, b_minus, a, 0], sp)
        from_sib.append(to_sibling(b_minus, a))
        down.wait_recv()
        half_m = move(xf.at[core, b_plus, a, 1], sm)
        from_sib.append(to_sibling(b_plus, a))
        opposite.append((a, half_p, half_m))

    relay(beside[0])
    far_p.wait_recv()
    far_m.wait_recv()
    beside.append((a_far, move(unit(second, a_far), sp), move(unit(second, a_far), sm)))
    from_sib.append(to_sibling(second, a_far))

    def finish(entry):
        a, half_p, half_m = entry
        half_p.wait_recv()
        half_m.wait_recv()
        from_sib.append(to_sibling(b_far, a))

    for n in range(1, 4):
        relay(beside[n])
        finish(opposite[n - 1])
    finish(opposite[3])
    row_b.wait_recv()
    for copy in get_w:
        copy.wait()
    for copy in from_sib:
        copy.wait_recv()

    gacc[...] = jnp.zeros_like(gacc)
    uacc[...] = jnp.zeros_like(uacc)

    def up_step(k, carry):
        rows = xf[k // 4, :, :, :, :, cols(k % 4, 512)].reshape(512, 512)
        gacc[...] += jnp.dot(rows, wg[cols(k, 512), :], preferred_element_type=F32)
        uacc[...] += jnp.dot(rows, wu[cols(k, 512), :], preferred_element_type=F32)
        return carry

    lax.fori_loop(0, 8, up_step, 0)
    gate = gacc[...]
    hid[...] = (gate / (1.0 + jnp.exp(-gate)) * uacc[...]).astype(BF)

    def down_step(half, out):
        def step(n, carry):
            part = jnp.dot(hid[...], wd[half, :, cols(n, 512)], preferred_element_type=F32)
            out[:, :, :, :, cols(n, 512)] = part.astype(BF).reshape(NX, NX, 2, CAP, 512)
            return carry

        lax.fori_loop(0, 4, step, 0)

    down_step(1 - core, ps)
    shares = {}
    for name, a in (("far", a_far), ("plus", a_plus), ("minus", a_minus), ("own", first)):
        shares[name] = send(ps.at[:, a], pr.at[a], sib)
    down_step(core, po)

    def both(b, a):
        return po[b, a].astype(F32) + pr[b, a].astype(F32)

    shares["far"].wait_recv()
    for a in range(4):
        s0[a] = both(b_far, a).astype(BF)
        if a == 1:
            hop_p = send(s0.at[pl.ds(0, 2)], r0.at[0], sp)
    hop_m = send(s0.at[pl.ds(2, 2)], r0.at[1], sm)
    shares["plus"].wait_recv()
    for a in (2, 3):
        s1[0, a] = both(b_plus, a).astype(BF)
    last = [send(s1.at[0, pl.ds(2, 2)], r1.at[0, pl.ds(2, 2)], sp)]
    shares["minus"].wait_recv()
    for a in (0, 1):
        s1[1, a] = both(b_minus, a).astype(BF)
    last.append(send(s1.at[1, pl.ds(0, 2)], r1.at[1, pl.ds(0, 2)], sm))
    hop_p.wait_recv()
    for a in (0, 1):
        s1[0, a] = (both(b_plus, a) + r0[0, a].astype(F32)).astype(BF)
    last.append(send(s1.at[0, pl.ds(0, 2)], r1.at[0, pl.ds(0, 2)], sp))
    hop_m.wait_recv()
    for a in (2, 3):
        s1[1, a] = (both(b_minus, a) + r0[1, a - 2].astype(F32)).astype(BF)
    last.append(send(s1.at[1, pl.ds(2, 2)], r1.at[1, pl.ds(2, 2)], sm))

    shares["own"].wait_recv()
    for copy in last:
        copy.wait_recv()

    def summed(a):
        return both(second, a) + r1[0, a].astype(F32) + r1[1, a].astype(F32)

    yb[0] = summed(a_far).astype(BF)
    end_p = send(yb.at[0, 0], q0.at[0], fp)
    end_m = send(yb.at[0, 1], q0.at[1], fm)
    plus = summed(a_plus)
    z1[0, 1] = plus[1].astype(BF)
    ends = [send(z1.at[0, 1], q1.at[0, 1], fp)]
    minus = summed(a_minus)
    z1[1, 0] = minus[0].astype(BF)
    ends.append(send(z1.at[1, 0], q1.at[1, 0], fm))
    end_p.wait_recv()
    z1[0, 0] = (plus[0] + q0[0].astype(F32)).astype(BF)
    ends.append(send(z1.at[0, 0], q1.at[0, 0], fp))
    end_m.wait_recv()
    z1[1, 1] = (minus[1] + q0[1].astype(F32)).astype(BF)
    ends.append(send(z1.at[1, 1], q1.at[1, 1], fm))
    yb[1] = summed(first).astype(BF)
    for copy in ends:
        copy.wait_recv()

    def whole(event):
        return (
            yb[1, event].astype(F32) + q1[0, event].astype(F32) + q1[1, event].astype(F32)
        ).astype(BF)

    vf[...] = whole(1 - core)
    other = send(vf, vv.at[core, z], sib)
    vv[core, z] = whole(core)

    class Ring:
        def __init__(self, ref, longer):
            self.ref = ref
            self.longer = longer
            self.up = send(ref(z), ref(z), zp)
            self.down = send(ref(z), ref(z), zm)
            self.step = 1

        def relay(self):
            n = self.step
            self.step += 1
            if n < 4 or self.longer != "down":
                self.up.wait_recv()
            if n < 4 or self.longer != "up":
                self.down.wait_recv()
            if n >= 4:
                return
            below, above = (z + NZ - n) % NZ, (z + n) % NZ
            if n < 3 or self.longer == "up":
                self.up = send(self.ref(below), self.ref(below), zp)
            elif self.longer == "both":
                self.up = send(self.ref(below, 0), self.ref(below, 0), zp)
            if n < 3 or self.longer == "down":
                self.down = send(self.ref(above), self.ref(above), zm)
            elif self.longer == "both":
                self.down = send(self.ref(above, 1), self.ref(above, 1), zm)

    rings = [Ring(lambda e: vv.at[core, e], "up")]
    other.wait_recv()
    rings.append(Ring(lambda e: vv.at[1 - core, e], "down"))

    get_k.wait()
    for copy in key_copies:
        copy.wait_recv()
    kept = jnp.dot(sa[0], ka[0], preferred_element_type=F32)
    for s in range(1, NZ):
        kept += jnp.dot(sa[s], ka[s], preferred_element_type=F32)
    kk[z] = kept.astype(BF).reshape(2, TOK // 2, GRP)
    rings.append(
        Ring(lambda e, half=None: kk.at[e] if half is None else kk.at[e, half], "both")
    )

    get_q.wait()
    for copy in query_copies:
        copy.wait_recv()

    def attend(n, carry):
        i, h = n // 4, n % 4
        query = qa[i, :, cols(h, HEAD)]
        top = jnp.full((1, TOK), NEG, F32)
        tiles = []
        for j in range(NZ):
            s = nt(ka[j, :, cols(h, HEAD)], query)
            s = jnp.where(mb[j, pl.ds(i, 1), :] > 0.5, s, NEG)
            top = jnp.maximum(top, jnp.max(s, axis=0, keepdims=True))
            tiles.append(s)
        top = top * SCALE
        total = jnp.zeros((1, TOK), F32)
        for s in tiles:
            w = jnp.exp(s * SCALE - top).astype(BF).astype(F32)
            total += jnp.sum(w, axis=0, keepdims=True)
        st[i, pl.ds(h, 1), :] = top
        st[i, pl.ds(h + 4, 1), :] = total
        return carry

    lax.fori_loop(0, 12, attend, 0)
    for ring in rings:
        ring.relay()
    lax.fori_loop(12, 22, attend, 0)
    for ring in rings:
        ring.relay()
    lax.fori_loop(22, 32, attend, 0)
    stat_copies = []
    for d in range(1, NZ):
        to = (z + d) % NZ
        stat_copies.append(send(st.at[to], sr.at[z], {"type": to}))
    sr[z] = st[z]
    for ring in rings:
        ring.relay()

    open_slots = jnp.zeros((TOK, TOK), F32)
    for s in range(NZ):
        open_slots += sa[s].astype(F32) * mb[s, pl.ds(z, 1), :]
    okm[...] = jnp.broadcast_to(jnp.sum(open_slots, axis=1, keepdims=True), (TOK, TOK))

    get_qs.wait()
    for copy in stat_copies:
        copy.wait_recv()
    rings[2].relay()

    def weigh(g, carry):
        keys = kk[g].reshape(TOK, GRP)
        query = qs[:, cols(g, GRP)]
        for h in range(4):
            at = slice(h * HEAD, (h + 1) * HEAD)
            s = nt(keys[:, at], query[:, at]) * SCALE - sr[g, h : h + 1, :]
            wts[g * 4 + h] = jnp.where(okm[...] > 0.5, jnp.exp(s), 0.0).astype(BF)
        return carry

    lax.fori_loop(0, NZ, weigh, 0)
    stats = sr[...].reshape(NZ * 8, TOK)
    inverse = 1.0 / jnp.concatenate([stats, stats], axis=0).T
    rings[0].relay()
    rings[1].relay()

    for h in range(2):
        values = vv[h].reshape(TOK, HALF)
        oe[:, h * HALF : (h + 1) * HALF] = tn(sa[z], values).astype(BF)
    put_e = fetch(oe, oe_out)
    for head in range(32):
        h, at = head // 16, (head % 16) * HEAD
        values = vv[h, :, :, at : at + HEAD].reshape(TOK, HEAD)
        column = (head // 4) * 8 + 4 + head % 4
        mixed = tn(wts[head], values) * inverse[:, column : column + 1]
        oa[:, head * HEAD : (head + 1) * HEAD] = mixed.astype(BF)
    put_a = fetch(oa, oa_out)
    for copy in started:
        copy.wait_send()
    put_e.wait()
    put_a.wait()


def on_device(tokens, token_types, tile_mask, queries, keys, gate_weight, up_weight, down_weight):
    meta = jnp.concatenate(
        [
            token_types.reshape(1, TOK),
            jnp.pad(tile_mask.reshape(1, NZ), ((0, 0), (0, TOK - NZ))),
            jnp.zeros((6, TOK), jnp.int32),
        ],
        axis=0,
    )
    anywhere = pl.BlockSpec(memory_space=pl.ANY)

    def vmem(*shape, dtype=BF):
        return pltpu.VMEM(shape, dtype)

    return pl.pallas_call(
        kernel,
        out_shape=[jax.ShapeDtypeStruct((TOK, D), BF)] * 2,
        in_specs=[anywhere] * 7,
        out_specs=[anywhere] * 2,
        scratch_shapes=[
            vmem(NZ, 8, TOK, dtype=jnp.int32),
            vmem(TOK, D),
            vmem(TOK, D),
            vmem(NZ, TOK, GRP),
            vmem(NZ, TOK, GRP),
            vmem(NZ, TOK, TOK),
            vmem(NZ, NZ, TOK, dtype=F32),
            vmem(2, NZ, CAP, HALF),
            vmem(2, 2, 4, CAP, HALF),
            vmem(2, 2, 3, CAP, HALF),
            vmem(2, NX, NX, 2, CAP, HALF),
            vmem(D, FFB),
            vmem(D, FFB),
            vmem(2, FFB, HALF),
            vmem(512, FFB, dtype=F32),
            vmem(512, FFB, dtype=F32),
            vmem(512, FFB),
            vmem(NX, NX, 2, CAP, HALF),
            vmem(NX, NX, 2, CAP, HALF),
            vmem(NX, NX, 2, CAP, HALF),
            vmem(NX, 2, CAP, HALF),
            vmem(2, 2, 2, CAP, HALF),
            vmem(2, NX, 2, CAP, HALF),
            vmem(2, NX, 2, CAP, HALF),
            vmem(2, 2, CAP, HALF),
            vmem(2, CAP, HALF),
            vmem(2, 2, CAP, HALF),
            vmem(2, 2, CAP, HALF),
            vmem(CAP, HALF),
            vmem(2, NZ, CAP, HALF),
            vmem(NZ, 2, TOK // 2, GRP),
            vmem(NZ, 8, TOK, dtype=F32),
            vmem(NZ, 8, TOK, dtype=F32),
            vmem(32, TOK, TOK),
            vmem(TOK, TOK, dtype=F32),
            vmem(TOK, D),
            vmem(TOK, D),
            pltpu.SemaphoreType.DMA((N_SEM,)),
            pltpu.SemaphoreType.DMA((N_SEM,)),
            pltpu.SemaphoreType.DMA((12,)),
        ],
        compiler_params=pltpu.CompilerParams(
            collective_id=0, has_side_effects=True, vmem_limit_bytes=60 * 1024 * 1024
        ),
    )(meta, tokens, queries, keys, gate_weight, up_weight, down_weight)


def solution(mesh):
    return jax.shard_map(
        on_device,
        mesh=mesh,
        in_specs=(
            P(("dp", "type"), None),
            P(("dp", "type"), None),
            P("dp", "type", None),
            P(("dp", "type"), None),
            P(("dp", "type"), None),
            P("type", None, "dp"),
            P("type", None, "dp"),
            P("type", "dp", None),
        ),
        out_specs=(P(("dp", "type"), None), P(("dp", "type"), None)),
        check_vma=False,
    )
```
